256 devices in a mesh: row: 8 (over x, core), col: 32 (over y, z).
Axes of the slice: x: 4, y: 4, z: 8, core: 2. Of those that a mesh axis runs over, the one named last changes fastest.
Arguments:
- src_coords: int32 [3, 131072], P(None, 'row'), may hold values from 0 to 51
- tgt_coords: int32 [3, 262144], P(None, 'col'), may hold values from 0 to 51
- src_mass: int32 [131072], P('row'), may hold values from 1 to 298
- tgt_mass: int32 [262144], P('col'), may hold values from 1 to 298
- tgt_start: float32 [262144], P('col'), may hold values from -10 to 170
- kept_src: int32 [8, 32, 64], P('row', 'col'), may hold values from 0 to 127, as said below
- kept_tgt: int32 [8, 32, 64], P('row', 'col'), may hold values from 0 to 63, as said below
- kept_count: int32 [8, 32], P('row', 'col'), may hold values from 1 to 64, as said below
Outputs:
- src_potential: float32 [131072], P('row')
- tgt_potential: float32 [262144], P('col')
The draws below stay inside these ranges and needn't reach their ends.
Inputs may be any that keep to these rules, and one draw needn't show every extreme that they name: `kept_src`: every source tile lies in a live pair of some device of its row block. Slots at or past a device's count hold pairs that are not live. `kept_tgt`: every target tile lies in a live pair of some device of its column block. `kept_count`: some device has exactly 64 live slots in every draw.
All inputs are finite; a program needn't handle non-finite values.
Results may differ from the reference program's by a relative error of at most 0.0001.
Values sent between devices are 32-bit elements; how exact they have to be, the bound alone decides.
No kernel may reach another device: no remote copies, remote signals or barrier semaphores. Data moves between devices by JAX's collectives and lax.ppermute only.
A program may use at most 64 MiB of HBM per device.

```python
import jax
import jax.numpy as jnp
from jax import lax

S_ROW = 16384
T_COL = 8192
KMAX = 64
ITERS = 3
NS = 131072
NT = 262144
N_ROW = 8
N_COL = 32


def cluster_coords(key, voxel_count):
    centre_key, spread_key = jax.random.split(key)
    centres = jax.random.randint(centre_key, (3, voxel_count // 128, 1), 6, 46)
    spread = jax.random.randint(spread_key, (3, voxel_count // 128, 128), -6, 7)
    coords = (centres + spread).reshape(3, voxel_count).astype(jnp.int32)
    coords = coords.at[:, 0].set(0)
    coords = coords.at[:, voxel_count - 1].set(51)
    return coords.astype(jnp.int32)


def rising_mass(key, voxel_count):
    ceiling = 100 + 200 * jnp.arange(voxel_count, dtype=jnp.int32) // voxel_count
    mass = jax.random.randint(key, (voxel_count,), 1, ceiling).astype(jnp.int32)
    mass = mass.at[0].set(1)
    mass = mass.at[voxel_count - 1].set(298)
    return mass.astype(jnp.int32)


def tile_pattern(key):
    base_key = jax.random.fold_in(key, 77)
    rank_key, extra_key, chosen_key = jax.random.split(base_key, 3)
    src_tiles_count = S_ROW // 128
    tgt_tiles_count = T_COL // 128
    cells = src_tiles_count * tgt_tiles_count
    row_index = jnp.arange(N_ROW, dtype=jnp.int32)[:, None, None]
    col_index = jnp.arange(N_COL, dtype=jnp.int32)[None, :, None]
    cell_index = jnp.arange(cells, dtype=jnp.int32)[None, None, :]
    src_cell = cell_index // tgt_tiles_count
    tgt_cell = cell_index % tgt_tiles_count
    needed = (src_cell % N_COL == col_index) & (tgt_cell == src_cell // N_COL % tgt_tiles_count)
    needed = needed | (tgt_cell % N_ROW == row_index) & (src_cell == tgt_cell // N_ROW % src_tiles_count)
    ranking = jax.random.randint(rank_key, (N_ROW, N_COL, cells), 0, cells)
    priority = jnp.where(needed, 0, 1 + ranking) * cells + cell_index
    ordered = jnp.argsort(priority, axis=-1, stable=True)[:, :, :KMAX].astype(jnp.int32)
    needed_count = jnp.sum(needed.astype(jnp.int32), axis=-1)
    extra = jax.random.randint(extra_key, (N_ROW, N_COL), 0, KMAX + 1)
    extra = extra * extra * extra // (KMAX * KMAX)
    counted = jnp.maximum(jnp.minimum(needed_count + extra, KMAX), 1)
    position = jnp.arange(N_ROW * N_COL, dtype=jnp.int32).reshape(N_ROW, N_COL)
    chosen = jax.random.randint(chosen_key, (), 0, N_ROW * N_COL)
    counted = jnp.where(position == chosen, KMAX, counted).astype(jnp.int32)
    return ((ordered // tgt_tiles_count).astype(jnp.int32), (ordered % tgt_tiles_count).astype(jnp.int32), counted)


def draw_src_coords(key, part):
    return cluster_coords(jax.random.fold_in(key, 11), NS)


def draw_tgt_coords(key, part):
    return cluster_coords(jax.random.fold_in(key, 13), NT)


def draw_src_mass(key, part):
    return rising_mass(jax.random.fold_in(key, 21), NS)


def draw_tgt_mass(key, part):
    return rising_mass(jax.random.fold_in(key, 23), NT)


def draw_tgt_start(key, part):
    first_key = jax.random.fold_in(jax.random.fold_in(key, 41), 0)
    return jnp.clip(3.0 * jax.random.normal(first_key, (NT,), jnp.float32), -9.0, 9.0)


def draw_kept_src(key, part):
    return tile_pattern(key)[0]


def draw_kept_tgt(key, part):
    return tile_pattern(key)[1]


def draw_kept_count(key, part):
    return tile_pattern(key)[2]


def setup_inputs(seed: int = 0) -> dict:
    keys = jax.random.split(jax.random.key(seed), 9)
    src_coords = draw_src_coords(jax.random.fold_in(keys[8], 71), 0)
    tgt_coords = draw_tgt_coords(jax.random.fold_in(keys[8], 71), 0)
    src_mass = draw_src_mass(jax.random.fold_in(keys[8], 71), 0)
    tgt_mass = draw_tgt_mass(jax.random.fold_in(keys[8], 71), 0)
    tgt_start = draw_tgt_start(jax.random.fold_in(keys[8], 71), 0)
    kept_src = draw_kept_src(jax.random.fold_in(keys[8], 71), 0)
    kept_tgt = draw_kept_tgt(jax.random.fold_in(keys[8], 71), 0)
    kept_count = draw_kept_count(jax.random.fold_in(keys[8], 71), 0)
    return dict(src_coords=src_coords, tgt_coords=tgt_coords, src_mass=src_mass, tgt_mass=tgt_mass, tgt_start=tgt_start, kept_src=kept_src, kept_tgt=kept_tgt, kept_count=kept_count)


very_negative = -1.0e30
cost_scale = 0.05


def tile_costs(src_grid, tgt_grid, src_ids, tgt_ids):
    src_tiles = jnp.take(src_grid, src_ids, axis=1).astype(jnp.float32)
    tgt_tiles = jnp.take(tgt_grid, tgt_ids, axis=1).astype(jnp.float32)
    square = None
    for component in range(3):
        difference = src_tiles[component][:, :, None] - tgt_tiles[component][:, None, :]
        square = difference * difference if component == 0 else square + difference * difference
    return cost_scale * square


def slot_partials(scores, live_slots, reduce_dim):
    peak_values = jnp.max(scores, axis=reduce_dim)
    totals = jnp.sum(jnp.exp(scores - jnp.expand_dims(peak_values, reduce_dim)), axis=reduce_dim)
    return jnp.where(live_slots[:, None], peak_values, very_negative), jnp.where(live_slots[:, None], totals, 0.0)


def segment_lse(peak_values, totals, tile_ids, tile_count):
    flat_ids = tile_ids.reshape(-1)
    peak_flat = peak_values.reshape(-1, 128)
    total_flat = totals.reshape(-1, 128)
    tile_peak = jax.ops.segment_max(peak_flat, flat_ids, num_segments=tile_count)
    weighted = total_flat * jnp.exp(peak_flat - tile_peak[flat_ids])
    tile_total = jax.ops.segment_sum(weighted, flat_ids, num_segments=tile_count)
    return tile_peak.reshape(-1) + jnp.log(tile_total.reshape(-1))


def reference(src_coords, tgt_coords, src_mass, tgt_mass, tgt_start, kept_src, kept_tgt, kept_count):
    src_tiles_count = S_ROW // 128
    tgt_tiles_count = T_COL // 128
    row_index = jnp.arange(N_ROW, dtype=jnp.int32)[:, None, None]
    col_index = jnp.arange(N_COL, dtype=jnp.int32)[None, :, None]
    global_src = (row_index * src_tiles_count + kept_src).reshape(N_ROW * N_COL, KMAX).astype(jnp.int32)
    global_tgt = (col_index * tgt_tiles_count + kept_tgt).reshape(N_ROW * N_COL, KMAX).astype(jnp.int32)
    live_all = (jnp.arange(KMAX, dtype=jnp.int32)[None, None, :] < kept_count[:, :, None]).reshape(N_ROW * N_COL, KMAX)
    src_weight = src_mass.astype(jnp.float32)
    tgt_weight = tgt_mass.astype(jnp.float32)
    src_log = jnp.log(src_weight) - jnp.log(jnp.sum(src_weight))
    tgt_log = jnp.log(tgt_weight) - jnp.log(jnp.sum(tgt_weight))
    src_grid = src_coords.reshape(3, NS // 128, 128)
    tgt_grid = tgt_coords.reshape(3, NT // 128, 128)
    tgt_potential = tgt_start
    src_potential = None
    for iteration in range(ITERS):
        tgt_table = tgt_potential.reshape(-1, 128)

        def row_terms(batch):
            ids_src, ids_tgt, live_slots = batch
            cost = tile_costs(src_grid, tgt_grid, ids_src, ids_tgt)
            picked = jnp.take(tgt_table, ids_tgt, axis=0)
            return slot_partials(picked[:, None, :] - cost, live_slots, 2)

        peak_values, totals = lax.map(row_terms, (global_src, global_tgt, live_all))
        src_potential = src_log - segment_lse(peak_values, totals, global_src, NS // 128)
        src_table = src_potential.reshape(-1, 128)

        def col_terms(batch):
            ids_src, ids_tgt, live_slots = batch
            cost = tile_costs(src_grid, tgt_grid, ids_src, ids_tgt)
            picked = jnp.take(src_table, ids_src, axis=0)
            return slot_partials(picked[:, :, None] - cost, live_slots, 1)

        peak_values, totals = lax.map(col_terms, (global_src, global_tgt, live_all))
        tgt_potential = tgt_log - segment_lse(peak_values, totals, global_tgt, NT // 128)
    return src_potential, tgt_potential
```

```python
import functools

import jax
import jax.numpy as jnp
from jax import lax
from jax.experimental import pallas as pl
from jax.experimental.pallas import tpu as pltpu
from jax.sharding import PartitionSpec as P

ITERS = 3
NONE = -1.0e30
UNITS = 20.0
STEP = 0.05
GROUP = 8


def lse(parts):
    top = functools.reduce(jnp.maximum, parts)
    terms = [jnp.exp(p - top) for p in parts]
    while len(terms) > 1:
        half = len(terms) // 2
        terms = [terms[k] + terms[k + half] for k in range(half)]
    return top + jnp.log(terms[0])


def features(coords):
    tiles = coords.reshape(3, -1, 1, 128)
    x, y, z = tiles[0], tiles[1], tiles[2]
    norm = x * x + y * y + z * z
    low = norm & 31
    high = norm - low
    one = jnp.ones_like(x)
    row = lax.broadcasted_iota(jnp.int32, (1, 16, 1), 1)

    def form(values):
        out = jnp.zeros((x.shape[0], 16, 128), jnp.int32)
        for index, value in enumerate(values):
            out = jnp.where(row == index, value, out)
        return out.astype(jnp.float32).astype(jnp.bfloat16)

    left = form([x, y, z, high, low, one, one])
    right = form([-2 * x, -2 * y, -2 * z, one, one, high, low])
    left = left.reshape(-1, 128, 128).transpose(0, 2, 1)
    return left, right


def half_step(potential, lane_ids_ref, sub_ids_ref, count_ref, left_ref, right_ref, peaks_ref, totals_ref, tops_ref, sums_ref, out_ref):
    sub_tiles = potential.shape[0]
    lane_tiles = tops_ref.shape[0]
    scaled = potential * UNITS
    if sub_tiles < 128:
        scaled = jnp.concatenate([scaled, jnp.zeros((128 - sub_tiles, 128), jnp.float32)], axis=0)
    columns = scaled.T
    count = count_ref[0, 0]
    peaks_ref[...] = jnp.full(peaks_ref.shape, NONE, jnp.float32)
    totals_ref[...] = jnp.ones(totals_ref.shape, jnp.float32)

    def group(g, carry):
        peaks, totals = [], []
        for u in range(GROUP):
            k = g * GROUP + u
            sub = sub_ids_ref[0, 0, k] & (sub_tiles - 1)
            lane = lane_ids_ref[0, 0, k] & (lane_tiles - 1)
            left = left_ref[sub >> 3]
            block = right_ref[lane]
            member = sub & 7
            right = jnp.concatenate(
                [jnp.where(member == q, block, jnp.zeros_like(block)) for q in range(8)], axis=0
            )
            square = jnp.dot(left, right, preferred_element_type=jnp.float32)
            value = jnp.take_along_axis(columns, jnp.full((128, 128), sub, jnp.int32), axis=1)
            score = value - square
            peak = jnp.max(score, axis=0, keepdims=True)
            total = jnp.sum(jnp.exp((score - peak) * STEP), axis=0, keepdims=True)
            peaks.append(jnp.where(k < count, peak * STEP, NONE))
            totals.append(total)
        start = pl.multiple_of(g * GROUP, GROUP)
        peaks_ref[pl.ds(start, GROUP), :] = jnp.concatenate(peaks, axis=0)
        totals_ref[pl.ds(start, GROUP), :] = jnp.concatenate(totals, axis=0)
        return carry

    lax.fori_loop(0, (count + (GROUP - 1)) // GROUP, group, 0)
    peaks_ref[...] = peaks_ref[...] + jnp.log(totals_ref[...])
    tops_ref[...] = jnp.full(tops_ref.shape, NONE, jnp.float32)
    sums_ref[...] = jnp.zeros(sums_ref.shape, jnp.float32)
    ids = [lane_ids_ref[0, 0, k] & (lane_tiles - 1) for k in range(64)]
    for k in range(64):
        at = pl.ds(ids[k], 1)
        tops_ref[at, :] = jnp.maximum(tops_ref[at, :], peaks_ref[k : k + 1, :])
    for k in range(64):
        totals_ref[k : k + 1, :] = jnp.exp(peaks_ref[k : k + 1, :] - tops_ref[pl.ds(ids[k], 1), :])
    for k in range(64):
        at = pl.ds(ids[k], 1)
        sums_ref[at, :] = sums_ref[at, :] + totals_ref[k : k + 1, :]
    sums = sums_ref[...]
    tops = tops_ref[...]
    out_ref[0:lane_tiles, :] = jnp.where(tops > 0.5 * NONE, tops + jnp.log(sums), NONE)


def put_total(out_ref, mass):
    rows = out_ref.shape[0]
    total = jnp.sum(jnp.sum(mass.astype(jnp.float32), axis=0, keepdims=True), axis=1, keepdims=True)
    out_ref[rows - 8 : rows, :] = jnp.broadcast_to(jnp.log(total), (8, 128))


def first_kernel(src_ids, tgt_ids, count, start, tgt_mass, left, right, out, peaks, totals, tops, sums):
    half_step(start[...], src_ids, tgt_ids, count, left, right, peaks, totals, tops, sums, out)
    put_total(out, tgt_mass[...])


def src_kernel(is_first, src_ids, tgt_ids, count, msg, src_mass, src_const, left, right, out, pot_ref, const_ref, peaks, totals, tops, sums):
    merged = lse([msg[k] for k in range(msg.shape[0])])
    const_ref[...] = merged[128:136]
    potential = jnp.log(src_mass[...].astype(jnp.float32)) - merged[0:128]
    if not is_first:
        potential = potential - src_const[0:1]
    pot_ref[...] = potential
    half_step(potential, tgt_ids, src_ids, count, left, right, peaks, totals, tops, sums, out)
    put_total(out, src_mass[...])


def tgt_value(is_first, parts, tgt_mass, tgt_const):
    merged = lse(parts)
    const = merged[64:72]
    potential = jnp.log(tgt_mass.astype(jnp.float32)) - tgt_const[0:1] - merged[0:64]
    if is_first:
        potential = potential + const[0:1]
    return potential, const


def tgt_kernel(is_first, src_ids, tgt_ids, count, m0, m1, m2, m3, tgt_mass, tgt_const, left, right, out, const_ref, peaks, totals, tops, sums):
    potential, const = tgt_value(is_first, [m0[...], m1[...], m2[...], m3[...]], tgt_mass[...], tgt_const[...])
    const_ref[...] = const
    half_step(potential, src_ids, tgt_ids, count, left, right, peaks, totals, tops, sums, out)
    put_total(out, tgt_mass[...])


SMEM = pl.BlockSpec(memory_space=pltpu.SMEM)
VMEM = pl.BlockSpec(memory_space=pltpu.VMEM)


def call(body, lane_tiles, extra_outs, *args):
    shape = jax.ShapeDtypeStruct
    return pl.pallas_call(
        body,
        out_shape=[shape((lane_tiles + 8, 128), jnp.float32)] + [shape(s, jnp.float32) for s in extra_outs],
        in_specs=[SMEM] * 3 + [VMEM] * (len(args) - 3),
        out_specs=[VMEM] * (1 + len(extra_outs)),
        scratch_shapes=[pltpu.VMEM((64, 128), jnp.float32)] * 2 + [pltpu.VMEM((lane_tiles, 128), jnp.float32)] * 2,
    )(*args)


def col_permute(value, shift):
    return lax.ppermute(value, "col", [(i, (i // 8 + shift) % 4 * 8 + i % 8) for i in range(32)])


def row_permute(value, shift):
    return lax.ppermute(value, "row", [(i, (i + 2 * shift) % 8) for i in range(8)])


Z_GROUPS = [[y * 8 + z for z in range(8)] for y in range(4)]


def over_col(message):
    merged = lse([message] + [col_permute(message, k) for k in (1, 2, 3)])
    copies = jnp.broadcast_to(merged[None], (8,) + merged.shape)
    return lax.all_to_all(copies, "col", 0, 0, tiled=True, axis_index_groups=Z_GROUPS)


def over_row(message):
    other = lax.ppermute(message, "row", [(i, i ^ 1) for i in range(8)])
    merged = lse([message, other])
    return [merged] + [row_permute(merged, k) for k in (1, 2, 3)]


def on_device(src_coords, tgt_coords, src_mass, tgt_mass, tgt_start, kept_src, kept_tgt, kept_count):
    src_mass = src_mass.reshape(128, 128)
    tgt_mass = tgt_mass.reshape(64, 128)
    src_left, src_right = features(src_coords)
    tgt_left, tgt_right = features(tgt_coords)
    lists = (kept_src, kept_tgt, kept_count)
    (message,) = call(first_kernel, 128, [], *lists, tgt_start.reshape(64, 128), tgt_mass, tgt_left, src_right)
    src_const = jnp.zeros((8, 128), jnp.float32)
    src_potential = None
    for iteration in range(ITERS):
        first = iteration == 0
        messages = over_col(message)
        message, src_potential, tgt_const = call(
            functools.partial(src_kernel, first), 64, [(128, 128), (8, 128)],
            *lists, messages, src_mass, src_const, src_left, tgt_right,
        )
        parts = over_row(message)
        if iteration + 1 < ITERS:
            message, src_const = call(
                functools.partial(tgt_kernel, first), 128, [(8, 128)],
                *lists, *parts, tgt_mass, tgt_const, tgt_left, src_right,
            )
    tgt_potential, _ = tgt_value(False, parts, tgt_mass, tgt_const)
    return src_potential.reshape(-1), tgt_potential.reshape(-1)


def solution(mesh):
    placed = (
        P(None, "row"),
        P(None, "col"),
        P("row"),
        P("col"),
        P("col"),
        P("row", "col", None),
        P("row", "col", None),
        P("row", "col"),
    )
    return jax.shard_map(
        on_device, mesh=mesh, in_specs=placed, out_specs=(P("row"), P("col")), check_vma=False
    )
```

```python
import functools

import jax
import jax.numpy as jnp
from jax import lax
from jax.experimental import pallas as pl
from jax.experimental.pallas import tpu as pltpu
from jax.sharding import PartitionSpec as P

ITERS = 3
NONE = -1.0e30
UNITS = 20.0
STEP = 0.05
BASE2 = STEP * 1.4426950408889634
SLOTS = 64


def lse(parts):
    top = functools.reduce(jnp.maximum, parts)
    terms = [jnp.exp(p - top) for p in parts]
    while len(terms) > 1:
        half = len(terms) // 2
        terms = [terms[k] + terms[k + half] for k in range(half)]
    return top + jnp.log(terms[0])


def features(coords_ref, rows_ref, left_out, right_out, scratch):
    tiles = coords_ref.shape[1] // 128
    for d in range(3):
        for t in range(tiles):
            rows_ref[d, t : t + 1, :] = coords_ref[d : d + 1, t * 128 : (t + 1) * 128]
    scratch[0 : tiles * 16, :] = jnp.zeros((tiles * 16, 128), jnp.float32)
    for at in range(0, tiles, 8):
        x, y, z = (rows_ref[d, at : at + 8, :] for d in range(3))
        norm = x * x + y * y + z * z
        low = norm & 31
        high = norm - low
        one = jnp.ones((8, 128), jnp.float32)
        if left_out is not None:
            values = [x, y, z, high, low, one, one]
        else:
            values = [-2 * x, -2 * y, -2 * z, one, one, high, low]
        for k, value in enumerate(values):
            scratch[pl.ds(at * 16 + k, 8, stride=16), :] = value.astype(jnp.float32)
    if left_out is not None:
        for c in range(tiles // 8):
            left_out[c] = scratch[c * 128 : (c + 1) * 128, :].T.astype(jnp.bfloat16)
    else:
        for t in range(tiles):
            right_out[t] = scratch[t * 16 : (t + 1) * 16, :].astype(jnp.bfloat16)


def half_step(potential, lane_ids_ref, sub_ids_ref, count_ref, left_ref, right_ref, peaks_ref, totals_ref, tops_ref, sums_ref, out_ref):
    sub_tiles = potential.shape[0]
    lane_tiles = tops_ref.shape[0]
    scaled = potential * UNITS
    if sub_tiles < 128:
        scaled = jnp.concatenate([scaled, jnp.zeros((128 - sub_tiles, 128), jnp.float32)], axis=0)
    columns = scaled.T
    count = count_ref[0, 0]
    ids = [lane_ids_ref[0, 0, k] & (lane_tiles - 1) for k in range(SLOTS)]
    peaks, totals = [], []
    for k in range(SLOTS):
        sub = sub_ids_ref[0, 0, k] & (sub_tiles - 1)
        block = right_ref[ids[k]]
        member = sub & 7
        right = jnp.concatenate(
            [jnp.where(member == q, block, jnp.zeros_like(block)) for q in range(8)], axis=0
        )
        square = jnp.dot(left_ref[sub >> 3], right, preferred_element_type=jnp.float32)
        value = jnp.take_along_axis(columns, jnp.full((128, 128), sub, jnp.int32), axis=1)
        score = value - square
        peak = jnp.max(score, axis=0, keepdims=True)
        totals.append(jnp.sum(jnp.exp2((score - peak) * BASE2), axis=0, keepdims=True))
        peaks.append(jnp.where(k < count, peak * STEP, NONE))
        if k % 8 == 7:
            peaks_ref[k - 7 : k + 1, :] = jnp.concatenate(peaks, axis=0) + jnp.log(jnp.concatenate(totals, axis=0))
            peaks, totals = [], []
    tops_ref[...] = jnp.full(tops_ref.shape, NONE, jnp.float32)
    sums_ref[...] = jnp.zeros(sums_ref.shape, jnp.float32)
    for k in range(SLOTS):
        at = pl.ds(ids[k], 1)
        tops_ref[at, :] = jnp.maximum(tops_ref[at, :], peaks_ref[k : k + 1, :])
    for k in range(SLOTS):
        totals_ref[k : k + 1, :] = jnp.exp(peaks_ref[k : k + 1, :] - tops_ref[pl.ds(ids[k], 1), :])
    for k in range(SLOTS):
        at = pl.ds(ids[k], 1)
        sums_ref[at, :] = sums_ref[at, :] + totals_ref[k : k + 1, :]
    tops = tops_ref[...]
    out_ref[0:lane_tiles, :] = jnp.where(tops > 0.5 * NONE, tops + jnp.log(sums_ref[...]), NONE)


def put_total(out_ref, mass):
    rows = out_ref.shape[0]
    total = jnp.sum(jnp.sum(mass.astype(jnp.float32), axis=0, keepdims=True), axis=1, keepdims=True)
    out_ref[rows - 8 : rows, :] = jnp.broadcast_to(jnp.log(total), (8, 128))


def first_kernel(src_ids, tgt_ids, count, start, tgt_mass, src_coords, tgt_coords, out, left, right, peaks, totals, tops, sums, rows, scratch):
    features(tgt_coords, rows, left, None, scratch)
    features(src_coords, rows, None, right, scratch)
    half_step(start[...], src_ids, tgt_ids, count, left, right, peaks, totals, tops, sums, out)
    put_total(out, tgt_mass[...])


def other_kernel(src_coords, tgt_coords, left, right, rows, scratch):
    features(src_coords, rows, left, None, scratch)
    features(tgt_coords, rows, None, right, scratch)


def src_kernel(is_first, src_ids, tgt_ids, count, msg, src_mass, src_const, left, right, out, pot_ref, const_ref, peaks, totals, tops, sums):
    merged = lse([msg[k] for k in range(msg.shape[0])])
    const_ref[...] = merged[128:136]
    potential = jnp.log(src_mass[...].astype(jnp.float32)) - merged[0:128]
    if not is_first:
        potential = potential - src_const[0:1]
    pot_ref[...] = potential
    half_step(potential, tgt_ids, src_ids, count, left, right, peaks, totals, tops, sums, out)
    put_total(out, src_mass[...])


def tgt_value(is_first, parts, tgt_mass, tgt_const):
    merged = lse(parts)
    const = merged[64:72]
    potential = jnp.log(tgt_mass.astype(jnp.float32)) - tgt_const[0:1] - merged[0:64]
    if is_first:
        potential = potential + const[0:1]
    return potential, const


def tgt_kernel(is_first, src_ids, tgt_ids, count, m0, m1, m2, m3, tgt_mass, tgt_const, left, right, out, const_ref, peaks, totals, tops, sums):
    potential, const = tgt_value(is_first, [m0[...], m1[...], m2[...], m3[...]], tgt_mass[...], tgt_const[...])
    const_ref[...] = const
    half_step(potential, src_ids, tgt_ids, count, left, right, peaks, totals, tops, sums, out)
    put_total(out, tgt_mass[...])


SMEM = pl.BlockSpec(memory_space=pltpu.SMEM)
VMEM = pl.BlockSpec(memory_space=pltpu.VMEM)


F32 = jnp.float32
FEATURE_SCRATCH = [pltpu.VMEM((3, 128, 128), jnp.int32), pltpu.VMEM((2048, 128), F32)]
PARAMS = pltpu.CompilerParams(vmem_limit_bytes=8 << 20)


def call(body, lane_tiles, extra_outs, *args, scratch=()):
    shapes = [jax.ShapeDtypeStruct((lane_tiles + 8, 128), F32)] + [jax.ShapeDtypeStruct(*s) for s in extra_outs]
    return pl.pallas_call(
        body,
        out_shape=shapes,
        in_specs=[SMEM] * 3 + [VMEM] * (len(args) - 3),
        out_specs=[VMEM] * len(shapes),
        scratch_shapes=[pltpu.VMEM((SLOTS, 128), F32)] * 2 + [pltpu.VMEM((lane_tiles, 128), F32)] * 2 + list(scratch),
        compiler_params=PARAMS,
    )(*args)


def feature_shapes(left_tiles, right_tiles):
    return [((left_tiles // 8, 128, 128), jnp.bfloat16), ((right_tiles, 16, 128), jnp.bfloat16)]


def other_features(src_coords, tgt_coords):
    shapes = [jax.ShapeDtypeStruct(*s) for s in feature_shapes(128, 64)]
    return pl.pallas_call(
        other_kernel, out_shape=shapes, in_specs=[VMEM] * 2, out_specs=[VMEM] * 2,
        scratch_shapes=FEATURE_SCRATCH, compiler_params=PARAMS,
    )(src_coords, tgt_coords)


def col_permute(value, shift):
    return lax.ppermute(value, "col", [(i, (i // 8 + shift) % 4 * 8 + i % 8) for i in range(32)])


def row_permute(value, shift):
    return lax.ppermute(value, "row", [(i, (i + 2 * shift) % 8) for i in range(8)])


Z_GROUPS = [[y * 8 + z for z in range(8)] for y in range(4)]


def over_col(message):
    merged = lse([message] + [col_permute(message, k) for k in (1, 2, 3)])
    copies = jnp.broadcast_to(merged[None], (8,) + merged.shape)
    return lax.all_to_all(copies, "col", 0, 0, tiled=True, axis_index_groups=Z_GROUPS)


def over_row(message):
    other = lax.ppermute(message, "row", [(i, i ^ 1) for i in range(8)])
    merged = lse([message, other])
    return [merged] + [row_permute(merged, k) for k in (1, 2, 3)]


def on_device(src_coords, tgt_coords, src_mass, tgt_mass, tgt_start, kept_src, kept_tgt, kept_count):
    src_mass = src_mass.reshape(128, 128)
    tgt_mass = tgt_mass.reshape(64, 128)
    lists = (kept_src, kept_tgt, kept_count)
    message, tgt_left, src_right = call(
        first_kernel, 128, feature_shapes(64, 128),
        *lists, tgt_start.reshape(64, 128), tgt_mass, src_coords, tgt_coords, scratch=FEATURE_SCRATCH,
    )
    src_left, tgt_right = other_features(src_coords, tgt_coords)
    src_const = jnp.zeros((8, 128), F32)
    src_potential = None
    for iteration in range(ITERS):
        first = iteration == 0
        messages = over_col(message)
        message, src_potential, tgt_const = call(
            functools.partial(src_kernel, first), 64, [((128, 128), F32), ((8, 128), F32)],
            *lists, messages, src_mass, src_const, src_left, tgt_right,
        )
        parts = over_row(message)
        if iteration + 1 < ITERS:
            message, src_const = call(
                functools.partial(tgt_kernel, first), 128, [((8, 128), F32)],
                *lists, *parts, tgt_mass, tgt_const, tgt_left, src_right,
            )
    tgt_potential, _ = tgt_value(False, parts, tgt_mass, tgt_const)
    return src_potential.reshape(-1), tgt_potential.reshape(-1)


def solution(mesh):
    placed = (
        P(None, "row"),
        P(None, "col"),
        P("row"),
        P("col"),
        P("col"),
        P("row", "col", None),
        P("row", "col", None),
        P("row", "col"),
    )
    return jax.shard_map(
        on_device, mesh=mesh, in_specs=placed, out_specs=(P("row"), P("col")), check_vma=False
    )
```

```python
import functools

import jax
import jax.numpy as jnp
from jax import lax
from jax.experimental import pallas as pl
from jax.experimental.pallas import tpu as pltpu
from jax.sharding import PartitionSpec as P

ITERS = 3
NONE = -1.0e30
UNITS = 20.0
STEP = 0.05
BASE2 = STEP * 1.4426950408889634
SLOTS = 64


def lse(parts):
    top = functools.reduce(jnp.maximum, parts)
    terms = [jnp.exp(p - top) for p in parts]
    while len(terms) > 1:
        half = len(terms) // 2
        terms = [terms[k] + terms[k + half] for k in range(half)]
    return top + jnp.log(terms[0])


def features(coords_ref, rows_ref, left_out, right_out, scratch):
    tiles = coords_ref.shape[1] // 128
    for d in range(3):
        for t in range(tiles):
            rows_ref[d, t : t + 1, :] = coords_ref[d : d + 1, t * 128 : (t + 1) * 128]
    scratch[0 : tiles * 16, :] = jnp.zeros((tiles * 16, 128), jnp.float32)
    for at in range(0, tiles, 8):
        x, y, z = (rows_ref[d, at : at + 8, :] for d in range(3))
        norm = x * x + y * y + z * z
        low = norm & 31
        high = norm - low
        one = jnp.ones((8, 128), jnp.float32)
        if left_out is not None:
            values = [x, y, z, high, low, one, one]
        else:
            values = [-2 * x, -2 * y, -2 * z, one, one, high, low]
        for k, value in enumerate(values):
            scratch[pl.ds(at * 16 + k, 8, stride=16), :] = value.astype(jnp.float32)
    if left_out is not None:
        for c in range(tiles // 8):
            left_out[c] = scratch[c * 128 : (c + 1) * 128, :].T.astype(jnp.bfloat16)
    else:
        for t in range(tiles):
            right_out[t] = scratch[t * 16 : (t + 1) * 16, :].astype(jnp.bfloat16)


def half_step(potential, lane_ids_ref, sub_ids_ref, count_ref, left_ref, right_ref, slots_ref, tops_ref, sums_ref, out_ref):
    sub_tiles = potential.shape[0]
    lane_tiles = tops_ref.shape[0] // 8
    scaled = potential * UNITS
    if sub_tiles < 128:
        scaled = jnp.concatenate([scaled, jnp.zeros((128 - sub_tiles, 128), jnp.float32)], axis=0)
    columns = scaled.T
    count = count_ref[0, 0]
    places = [pl.ds(pl.multiple_of(lane_ids_ref[0, 0, k] * 8, 8), 8) for k in range(SLOTS)]
    tops_ref[...] = jnp.full(tops_ref.shape, NONE, jnp.float32)
    sums_ref[...] = jnp.zeros(sums_ref.shape, jnp.float32)
    for k in range(SLOTS):
        sub = sub_ids_ref[0, 0, k]
        block = right_ref[lane_ids_ref[0, 0, k]]
        member = sub & 7
        right = jnp.concatenate(
            [jnp.where(member == q, block, jnp.zeros_like(block)) for q in range(8)], axis=0
        )
        square = jnp.dot(left_ref[sub >> 3], right, preferred_element_type=jnp.float32)
        value = jnp.take_along_axis(columns, jnp.full((128, 128), sub, jnp.int32), axis=1)
        score = (value - square).reshape(16, 8, 128)
        peak = jnp.max(score, axis=0)
        total = jnp.sum(jnp.exp2((score - peak[None]) * BASE2), axis=0)
        slots_ref[k * 8 : k * 8 + 8, :] = jnp.where(k < count, peak * STEP + jnp.log(total), NONE)
    for k in range(SLOTS):
        tops_ref[places[k], :] = jnp.maximum(tops_ref[places[k], :], slots_ref[k * 8 : k * 8 + 8, :])
    for k in range(SLOTS):
        at = slice(k * 8, k * 8 + 8)
        slots_ref[at, :] = jnp.exp(slots_ref[at, :] - tops_ref[places[k], :])
    for k in range(SLOTS):
        sums_ref[places[k], :] = sums_ref[places[k], :] + slots_ref[k * 8 : k * 8 + 8, :]
    for at in range(0, lane_tiles, 8):
        tops = [tops_ref[pl.ds(at * 8 + q, 8, stride=8), :] for q in range(8)]
        sums = [sums_ref[pl.ds(at * 8 + q, 8, stride=8), :] for q in range(8)]
        top = functools.reduce(jnp.maximum, tops)
        total = functools.reduce(jnp.add, [s * jnp.exp(t - top) for t, s in zip(tops, sums)])
        out_ref[at : at + 8, :] = jnp.where(top > 0.5 * NONE, top + jnp.log(total), NONE)


def put_total(out_ref, mass):
    rows = out_ref.shape[0]
    total = jnp.sum(jnp.sum(mass.astype(jnp.float32), axis=0, keepdims=True), axis=1, keepdims=True)
    out_ref[rows - 8 : rows, :] = jnp.broadcast_to(jnp.log(total), (8, 128))


def first_kernel(src_ids, tgt_ids, count, start, tgt_mass, src_coords, tgt_coords, out, left, right, slots, tops, sums, rows, scratch):
    features(tgt_coords, rows, left, None, scratch)
    features(src_coords, rows, None, right, scratch)
    half_step(start[...], src_ids, tgt_ids, count, left, right, slots, tops, sums, out)
    put_total(out, tgt_mass[...])


def other_kernel(src_coords, tgt_coords, left, right, rows, scratch):
    features(src_coords, rows, left, None, scratch)
    features(tgt_coords, rows, None, right, scratch)


def src_kernel(is_first, src_ids, tgt_ids, count, m0, m1, m2, m3, src_mass, src_const, left, right, out, pot_ref, const_ref, slots, tops, sums):
    merged = lse([m0[...], m1[...], m2[...], m3[...]])
    const_ref[...] = merged[128:136]
    potential = jnp.log(src_mass[...].astype(jnp.float32)) - merged[0:128]
    if not is_first:
        potential = potential - src_const[0:1]
    pot_ref[...] = potential
    half_step(potential, tgt_ids, src_ids, count, left, right, slots, tops, sums, out)
    put_total(out, src_mass[...])


def tgt_value(is_first, parts, tgt_mass, tgt_const):
    merged = lse(parts)
    const = merged[64:72]
    potential = jnp.log(tgt_mass.astype(jnp.float32)) - tgt_const[0:1] - merged[0:64]
    if is_first:
        potential = potential + const[0:1]
    return potential, const


def tgt_kernel(is_first, src_ids, tgt_ids, count, m0, m1, m2, m3, tgt_mass, tgt_const, left, right, out, const_ref, slots, tops, sums):
    potential, const = tgt_value(is_first, [m0[...], m1[...], m2[...], m3[...]], tgt_mass[...], tgt_const[...])
    const_ref[...] = const
    half_step(potential, src_ids, tgt_ids, count, left, right, slots, tops, sums, out)
    put_total(out, tgt_mass[...])


SMEM = pl.BlockSpec(memory_space=pltpu.SMEM)
VMEM = pl.BlockSpec(memory_space=pltpu.VMEM)


F32 = jnp.float32
FEATURE_SCRATCH = [pltpu.VMEM((3, 128, 128), jnp.int32), pltpu.VMEM((2048, 128), F32)]
PARAMS = pltpu.CompilerParams(vmem_limit_bytes=8 << 20)


def call(body, lane_tiles, extra_outs, *args, scratch=()):
    shapes = [jax.ShapeDtypeStruct((lane_tiles + 8, 128), F32)] + [jax.ShapeDtypeStruct(*s) for s in extra_outs]
    return pl.pallas_call(
        body,
        out_shape=shapes,
        in_specs=[SMEM] * 3 + [VMEM] * (len(args) - 3),
        out_specs=[VMEM] * len(shapes),
        scratch_shapes=[pltpu.VMEM((SLOTS * 8, 128), F32)] + [pltpu.VMEM((lane_tiles * 8, 128), F32)] * 2 + list(scratch),
        compiler_params=PARAMS,
    )(*args)


def feature_shapes(left_tiles, right_tiles):
    return [((left_tiles // 8, 128, 128), jnp.bfloat16), ((right_tiles, 16, 128), jnp.bfloat16)]


def other_features(src_coords, tgt_coords):
    shapes = [jax.ShapeDtypeStruct(*s) for s in feature_shapes(128, 64)]
    return pl.pallas_call(
        other_kernel, out_shape=shapes, in_specs=[VMEM] * 2, out_specs=[VMEM] * 2,
        scratch_shapes=FEATURE_SCRATCH, compiler_params=PARAMS,
    )(src_coords, tgt_coords)


def col_permute(value, shift):
    return lax.ppermute(value, "col", [(i, (i // 8 + shift) % 4 * 8 + i % 8) for i in range(32)])


def row_permute(value, shift):
    return lax.ppermute(value, "row", [(i, (i + 2 * shift) % 8) for i in range(8)])


def z_permute(value, shift):
    return lax.ppermute(value, "col", [(i, i // 8 * 8 + (i + shift) % 8) for i in range(32)])


def over_col(message):
    merged = lse([message] + [col_permute(message, k) for k in (1, 2, 3)])
    merged = lse([merged, z_permute(merged, 4)])
    return [merged] + [z_permute(merged, k) for k in (1, 2, 7)]


def over_row(message):
    other = lax.ppermute(message, "row", [(i, i ^ 1) for i in range(8)])
    merged = lse([message, other])
    return [merged] + [row_permute(merged, k) for k in (1, 2, 3)]


def on_device(src_coords, tgt_coords, src_mass, tgt_mass, tgt_start, kept_src, kept_tgt, kept_count):
    src_mass = src_mass.reshape(128, 128)
    tgt_mass = tgt_mass.reshape(64, 128)
    lists = (kept_src, kept_tgt, kept_count)
    message, tgt_left, src_right = call(
        first_kernel, 128, feature_shapes(64, 128),
        *lists, tgt_start.reshape(64, 128), tgt_mass, src_coords, tgt_coords, scratch=FEATURE_SCRATCH,
    )
    src_left, tgt_right = other_features(src_coords, tgt_coords)
    src_const = jnp.zeros((8, 128), F32)
    src_potential = None
    for iteration in range(ITERS):
        first = iteration == 0
        messages = over_col(message)
        message, src_potential, tgt_const = call(
            functools.partial(src_kernel, first), 64, [((128, 128), F32), ((8, 128), F32)],
            *lists, *messages, src_mass, src_const, src_left, tgt_right,
        )
        parts = over_row(message)
        if iteration + 1 < ITERS:
            message, src_const = call(
                functools.partial(tgt_kernel, first), 128, [((8, 128), F32)],
                *lists, *parts, tgt_mass, tgt_const, tgt_left, src_right,
            )
    tgt_potential, _ = tgt_value(False, parts, tgt_mass, tgt_const)
    return src_potential.reshape(-1), tgt_potential.reshape(-1)


def solution(mesh):
    placed = (
        P(None, "row"),
        P(None, "col"),
        P("row"),
        P("col"),
        P("col"),
        P("row", "col", None),
        P("row", "col", None),
        P("row", "col"),
    )
    return jax.shard_map(
        on_device, mesh=mesh, in_specs=placed, out_specs=(P("row"), P("col")), check_vma=False
    )
```

```python
import functools

import jax
import jax.numpy as jnp
from jax import lax
from jax.experimental import pallas as pl
from jax.experimental.pallas import tpu as pltpu
from jax.sharding import PartitionSpec as P

ITERS = 3
NONE = -1.0e30
LOG2E = 1.4426950408889634
LN2 = 0.6931471805599453
COST = 0.05 * LOG2E
SLOTS = 64
GROUP = 16
F32 = jnp.float32


def lse(parts):
    top = functools.reduce(jnp.maximum, parts)
    terms = [jnp.exp(p - top) for p in parts]
    while len(terms) > 1:
        half = len(terms) // 2
        terms = [terms[k] + terms[k + half] for k in range(half)]
    return top + jnp.log(terms[0])


def features(coords_ref, rows_ref, wide_ref, left_ref, right_ref):
    tiles = coords_ref.shape[1] // 128
    for d in range(3):
        for t in range(tiles):
            rows_ref[d, t : t + 1, :] = coords_ref[d : d + 1, t * 128 : (t + 1) * 128]
    wide_ref[0 : tiles * 16, :] = jnp.zeros((tiles * 16, 128), F32)
    for at in range(0, tiles, 8):
        x, y, z = (rows_ref[d, at : at + 8, :] for d in range(3))
        norm = x * x + y * y + z * z
        low = norm & 31
        high = norm - low
        one = jnp.ones((8, 128), F32)
        if right_ref is None:
            values = [x, y, z, high, low, one, one]
        else:
            values = [-2 * x, -2 * y, -2 * z, one, one, high, low]
        for k, value in enumerate(values):
            wide_ref[pl.ds(at * 16 + k, 8, stride=16), :] = value.astype(F32)
    if right_ref is None:
        for c in range(tiles // 8):
            left_ref[c] = wide_ref[c * 128 : (c + 1) * 128, :].T.astype(jnp.bfloat16)
    else:
        for t in range(tiles):
            right_ref[t] = wide_ref[t * 16 : (t + 1) * 16, :].astype(jnp.bfloat16)


def squares(sub_coords, lane_coords, sub_ids_ref, lane_ids_ref, rows_ref, wide_ref, left_ref, right_ref, out_ref):
    features(sub_coords, rows_ref, wide_ref, left_ref, None)
    features(lane_coords, rows_ref, wide_ref, None, right_ref)

    def some(g, carry):
        for u in range(GROUP):
            k = g * GROUP + u
            sub = sub_ids_ref[0, 0, k]
            block = right_ref[lane_ids_ref[0, 0, k]]
            member = sub & 7
            right = jnp.concatenate(
                [jnp.where(member == q, block, jnp.zeros_like(block)) for q in range(8)], axis=0
            )
            out_ref[k] = jnp.dot(left_ref[sub >> 3], right, preferred_element_type=F32) * COST
        return carry

    lax.fori_loop(0, SLOTS // GROUP, some, 0)


def half_step(potential, lane_ids_ref, sub_ids_ref, count_ref, square_ref, slots_ref, tops_ref, sums_ref, out_ref):
    sub_tiles = potential.shape[0]
    lane_tiles = tops_ref.shape[0] // 8
    scaled = potential * LOG2E
    if sub_tiles < 128:
        scaled = jnp.concatenate([scaled, jnp.zeros((128 - sub_tiles, 128), jnp.float32)], axis=0)
    columns = scaled.T
    count = count_ref[0, 0]
    places = [pl.ds(pl.multiple_of(lane_ids_ref[0, 0, k] * 8, 8), 8) for k in range(SLOTS)]
    tops_ref[...] = jnp.full(tops_ref.shape, NONE, jnp.float32)
    sums_ref[...] = jnp.zeros(sums_ref.shape, jnp.float32)
    for k in range(SLOTS):
        sub = sub_ids_ref[0, 0, k]
        value = jnp.take_along_axis(columns, jnp.full((128, 128), sub, jnp.int32), axis=1)
        score = (value - square_ref[k]).reshape(16, 8, 128)
        peak = jnp.max(score, axis=0)
        total = jnp.sum(jnp.exp2(score - peak[None]), axis=0)
        slots_ref[k * 8 : k * 8 + 8, :] = jnp.where(k < count, peak * LN2 + jnp.log(total), NONE)
    for k in range(SLOTS):
        tops_ref[places[k], :] = jnp.maximum(tops_ref[places[k], :], slots_ref[k * 8 : k * 8 + 8, :])
    for k in range(SLOTS):
        at = slice(k * 8, k * 8 + 8)
        slots_ref[at, :] = jnp.exp(slots_ref[at, :] - tops_ref[places[k], :])
    for k in range(SLOTS):
        sums_ref[places[k], :] = sums_ref[places[k], :] + slots_ref[k * 8 : k * 8 + 8, :]
    for at in range(0, lane_tiles, 8):
        tops = [tops_ref[pl.ds(at * 8 + q, 8, stride=8), :] for q in range(8)]
        sums = [sums_ref[pl.ds(at * 8 + q, 8, stride=8), :] for q in range(8)]
        top = functools.reduce(jnp.maximum, tops)
        total = functools.reduce(jnp.add, [s * jnp.exp(t - top) for t, s in zip(tops, sums)])
        out_ref[at : at + 8, :] = jnp.where(top > 0.5 * NONE, top + jnp.log(total), NONE)


def put_total(out_ref, mass):
    rows = out_ref.shape[0]
    total = jnp.sum(jnp.sum(mass.astype(F32), axis=0, keepdims=True), axis=1, keepdims=True)
    out_ref[rows - 8 : rows, :] = jnp.broadcast_to(jnp.log(total), (8, 128))


def first_kernel(src_list, tgt_list, count_list, start_in, mass_in, src_in, tgt_in, out, slots, tops, sums, rows, wide, left, right, src_ids, tgt_ids, count, start, mass, src_coords, tgt_coords, square, sems):
    pairs = [(src_list, src_ids), (tgt_list, tgt_ids), (count_list, count), (start_in, start), (mass_in, mass), (src_in, src_coords), (tgt_in, tgt_coords)]
    copies = [pltpu.make_async_copy(here, there, sems.at[n]) for n, (here, there) in enumerate(pairs)]
    for copy in copies:
        copy.start()
    for copy in copies:
        copy.wait()
    squares(tgt_coords, src_coords, tgt_ids, src_ids, rows, wide, left, right, square)
    half_step(start[...], src_ids, tgt_ids, count, square, slots, tops, sums, out)
    put_total(out, mass[...])


def square_kernel(sub_ids, lane_ids, sub_coords, lane_coords, square, rows, wide, left, right):
    squares(sub_coords, lane_coords, sub_ids, lane_ids, rows, wide, left, right, square)


def first_src_kernel(src_ids, tgt_ids, count, m0, m1, m2, m3, src_mass, square, out, tgt_const, slots, tops, sums):
    merged = lse([m0[...], m1[...], m2[...], m3[...]])
    tgt_const[...] = merged[128:136]
    potential = jnp.log(src_mass[...].astype(F32)) - merged[0:128]
    half_step(potential, tgt_ids, src_ids, count, square, slots, tops, sums, out)
    put_total(out, src_mass[...])


def src_kernel(src_ids, tgt_ids, count, m0, m1, m2, m3, src_mass, src_const, square, out, *rest):
    *pot, slots, tops, sums = rest
    potential = jnp.log(src_mass[...].astype(F32)) - src_const[0:1] - lse([m0[...], m1[...], m2[...], m3[...]])
    if pot:
        pot[0][...] = potential
    half_step(potential, tgt_ids, src_ids, count, square, slots, tops, sums, out)


def first_tgt_kernel(src_ids, tgt_ids, count, m0, m1, m2, m3, tgt_mass, tgt_const, square, out, src_const, slots, tops, sums):
    merged = lse([m0[...], m1[...], m2[...], m3[...]])
    src_const[...] = merged[64:72]
    potential = jnp.log(tgt_mass[...].astype(F32)) - tgt_const[0:1] - (merged[0:64] - merged[64:65])
    half_step(potential, src_ids, tgt_ids, count, square, slots, tops, sums, out)


def tgt_kernel(src_ids, tgt_ids, count, m0, m1, m2, m3, tgt_mass, tgt_const, square, out, slots, tops, sums):
    potential = jnp.log(tgt_mass[...].astype(F32)) - tgt_const[0:1] - lse([m0[...], m1[...], m2[...], m3[...]])
    half_step(potential, src_ids, tgt_ids, count, square, slots, tops, sums, out)


SMEM = pl.BlockSpec(memory_space=pltpu.SMEM)
VMEM = pl.BlockSpec(memory_space=pltpu.VMEM)


HBM = pl.BlockSpec(memory_space=pltpu.HBM)
PARAMS = pltpu.CompilerParams(vmem_limit_bytes=12 << 20)
SQUARES = jax.ShapeDtypeStruct((SLOTS, 128, 128), F32)


def half_scratch(lane_tiles):
    return [pltpu.VMEM((SLOTS * 8, 128), F32)] + [pltpu.VMEM((lane_tiles * 8, 128), F32)] * 2


def square_scratch(left_tiles, right_tiles):
    return [
        pltpu.VMEM((3, 128, 128), jnp.int32),
        pltpu.VMEM((2048, 128), F32),
        pltpu.VMEM((left_tiles // 8, 128, 128), jnp.bfloat16),
        pltpu.VMEM((right_tiles, 16, 128), jnp.bfloat16),
    ]


def first_call(*args):
    return pl.pallas_call(
        first_kernel,
        out_shape=jax.ShapeDtypeStruct((136, 128), F32),
        in_specs=[HBM] * 7,
        out_specs=VMEM,
        scratch_shapes=half_scratch(128) + square_scratch(64, 128)
        + [pltpu.SMEM(x.shape, x.dtype) for x in args[:3]]
        + [pltpu.VMEM(x.shape, x.dtype) for x in args[3:]]
        + [pltpu.VMEM(SQUARES.shape, F32), pltpu.SemaphoreType.DMA((7,))],
    )(*args)


def square_call(sub_ids, lane_ids, sub_coords, lane_coords):
    return pl.pallas_call(
        square_kernel, out_shape=SQUARES, in_specs=[SMEM] * 2 + [VMEM] * 2, out_specs=VMEM,
        scratch_shapes=square_scratch(sub_coords.shape[1] // 128, lane_coords.shape[1] // 128), compiler_params=PARAMS,
    )(sub_ids, lane_ids, sub_coords, lane_coords)


def call(body, lane_tiles, outs, *args):
    return pl.pallas_call(
        body,
        out_shape=[jax.ShapeDtypeStruct((rows, 128), F32) for rows in outs],
        in_specs=[SMEM] * 3 + [VMEM] * (len(args) - 3),
        out_specs=[VMEM] * len(outs),
        scratch_shapes=half_scratch(lane_tiles),
        compiler_params=PARAMS,
    )(*args)


def col_permute(value, source):
    pairs = []
    for i in range(32):
        y, z = source(i // 8, i % 8)
        pairs.append((y % 4 * 8 + z % 8, i))
    return lax.ppermute(value, "col", pairs)


def row_permute(value, shift):
    return lax.ppermute(value, "row", [(i, (i + 2 * shift) % 8) for i in range(8)])


def over_col(message):
    merged = lse([
        message,
        col_permute(message, lambda y, z: (y, z ^ 1)),
        col_permute(message, lambda y, z: (y ^ 1, z)),
        col_permute(message, lambda y, z: (y ^ 1, z ^ 1)),
    ])
    merged = lse([merged, col_permute(merged, lambda y, z: (y ^ 3, z))])
    return [merged] + [col_permute(merged, lambda y, z, k=k: (y, z + k if z % 2 else z - k)) for k in (1, 3, -2)]


def over_row(message):
    other = lax.ppermute(message, "row", [(i, i ^ 1) for i in range(8)])
    merged = lse([message, other])
    return [merged] + [row_permute(merged, k) for k in (1, 2, 3)]


def on_device(src_coords, tgt_coords, src_mass, tgt_mass, tgt_start, kept_src, kept_tgt, kept_count):
    src_mass = src_mass.reshape(128, 128)
    tgt_mass = tgt_mass.reshape(64, 128)
    lists = (kept_src, kept_tgt, kept_count)
    message = first_call(*lists, tgt_start.reshape(64, 128), tgt_mass, src_coords, tgt_coords)
    tgt_lanes = square_call(kept_src, kept_tgt, src_coords, tgt_coords)
    src_lanes = square_call(kept_tgt, kept_src, tgt_coords, src_coords)
    for iteration in range(ITERS):
        parts = over_col(message)
        if iteration == 0:
            message, tgt_const = call(first_src_kernel, 64, [72, 8], *lists, *parts, src_mass, tgt_lanes)
        elif iteration + 1 < ITERS:
            (message,) = call(src_kernel, 64, [64], *lists, *parts, src_mass, src_const, tgt_lanes)
        else:
            message, src_potential = call(src_kernel, 64, [64, 128], *lists, *parts, src_mass, src_const, tgt_lanes)
        parts = over_row(message)
        if iteration == 0:
            message, src_const = call(first_tgt_kernel, 128, [128, 8], *lists, *parts, tgt_mass, tgt_const, src_lanes)
        elif iteration + 1 < ITERS:
            (message,) = call(tgt_kernel, 128, [128], *lists, *parts, tgt_mass, tgt_const, src_lanes)
    tgt_potential = jnp.log(tgt_mass.astype(F32)) - tgt_const[0:1] - lse(parts)
    return src_potential.reshape(-1), tgt_potential.reshape(-1)


def solution(mesh):
    placed = (
        P(None, "row"),
        P(None, "col"),
        P("row"),
        P("col"),
        P("col"),
        P("row", "col", None),
        P("row", "col", None),
        P("row", "col"),
    )
    return jax.shard_map(
        on_device, mesh=mesh, in_specs=placed, out_specs=(P("row"), P("col")), check_vma=False
    )
```

```python
import functools

import jax
import jax.numpy as jnp
from jax import lax
from jax.experimental import pallas as pl
from jax.experimental.pallas import tpu as pltpu
from jax.sharding import PartitionSpec as P

ITERS = 3
NONE = -1.0e30
LOG2E = 1.4426950408889634
LN2 = 0.6931471805599453
COST = 0.05 * LOG2E
SLOTS = 64
GROUP = 16
F32 = jnp.float32


def lse(parts):
    top = functools.reduce(jnp.maximum, parts)
    terms = [jnp.exp(p - top) for p in parts]
    while len(terms) > 1:
        half = len(terms) // 2
        terms = [terms[k] + terms[k + half] for k in range(half)]
    return top + jnp.log(terms[0])


def features(coords_ref, rows_ref, wide_ref, left_ref, right_ref):
    tiles = coords_ref.shape[1] // 128
    for d in range(3):
        for t in range(tiles):
            rows_ref[d, t : t + 1, :] = coords_ref[d : d + 1, t * 128 : (t + 1) * 128]
    wide_ref[0 : tiles * 16, :] = jnp.zeros((tiles * 16, 128), F32)
    for at in range(0, tiles, 8):
        x, y, z = (rows_ref[d, at : at + 8, :] for d in range(3))
        norm = x * x + y * y + z * z
        low = norm & 31
        high = norm - low
        one = jnp.ones((8, 128), F32)
        if right_ref is None:
            values = [x, y, z, high, low, one, one]
        else:
            values = [-2 * x, -2 * y, -2 * z, one, one, high, low]
        for k, value in enumerate(values):
            wide_ref[pl.ds(at * 16 + k, 8, stride=16), :] = value.astype(F32)
    if right_ref is None:
        for c in range(tiles // 8):
            left_ref[c] = wide_ref[c * 128 : (c + 1) * 128, :].T.astype(jnp.bfloat16)
    else:
        for t in range(tiles):
            right_ref[t] = wide_ref[t * 16 : (t + 1) * 16, :].astype(jnp.bfloat16)


def squares(sub_coords, lane_coords, sub_ids_ref, lane_ids_ref, rows_ref, wide_ref, left_ref, right_ref, out_ref):
    features(sub_coords, rows_ref, wide_ref, left_ref, None)
    features(lane_coords, rows_ref, wide_ref, None, right_ref)

    def some(g, carry):
        for u in range(GROUP):
            k = g * GROUP + u
            sub = sub_ids_ref[0, 0, k]
            block = right_ref[lane_ids_ref[0, 0, k]]
            member = sub & 7
            right = jnp.concatenate(
                [jnp.where(member == q, block, jnp.zeros_like(block)) for q in range(8)], axis=0
            )
            out_ref[k] = jnp.dot(left_ref[sub >> 3], right, preferred_element_type=F32) * COST
        return carry

    lax.fori_loop(0, SLOTS // GROUP, some, 0)


def half_step(potential, lane_ids_ref, sub_ids_ref, count_ref, square_ref, table_ref, columns_ref, slots_ref, tops_ref, sums_ref, out_ref):
    sub_tiles = potential.shape[0]
    lane_tiles = tops_ref.shape[0] // 8
    scaled = potential * LOG2E
    high = scaled.astype(jnp.bfloat16).astype(F32)
    middle = (scaled - high).astype(jnp.bfloat16).astype(F32)
    low = scaled - high - middle
    empty = jnp.zeros((32, 128), F32)
    for c in range(sub_tiles // 32):
        at = slice(c * 32, c * 32 + 32)
        columns_ref[c] = jnp.concatenate([high[at], middle[at], low[at], empty], axis=0).T.astype(jnp.bfloat16)
    count = count_ref[0, 0]
    places = [pl.ds(pl.multiple_of(lane_ids_ref[0, 0, k] * 8, 8), 8) for k in range(SLOTS)]
    tops_ref[...] = jnp.full(tops_ref.shape, NONE, jnp.float32)
    sums_ref[...] = jnp.zeros(sums_ref.shape, jnp.float32)
    for k in range(SLOTS):
        sub = sub_ids_ref[0, 0, k]
        value = jnp.dot(columns_ref[sub >> 5], table_ref[sub & 31], preferred_element_type=F32)
        score = (value - square_ref[k]).reshape(16, 8, 128)
        peak = jnp.max(score, axis=0)
        total = jnp.sum(jnp.exp2(score - peak[None]), axis=0)
        slots_ref[k * 8 : k * 8 + 8, :] = jnp.where(k < count, peak * LN2 + jnp.log(total), NONE)
    for k in range(SLOTS):
        tops_ref[places[k], :] = jnp.maximum(tops_ref[places[k], :], slots_ref[k * 8 : k * 8 + 8, :])
    for k in range(SLOTS):
        at = slice(k * 8, k * 8 + 8)
        slots_ref[at, :] = jnp.exp(slots_ref[at, :] - tops_ref[places[k], :])
    for k in range(SLOTS):
        sums_ref[places[k], :] = sums_ref[places[k], :] + slots_ref[k * 8 : k * 8 + 8, :]
    for at in range(0, lane_tiles, 8):
        tops = [tops_ref[pl.ds(at * 8 + q, 8, stride=8), :] for q in range(8)]
        sums = [sums_ref[pl.ds(at * 8 + q, 8, stride=8), :] for q in range(8)]
        top = functools.reduce(jnp.maximum, tops)
        total = functools.reduce(jnp.add, [s * jnp.exp(t - top) for t, s in zip(tops, sums)])
        out_ref[at : at + 8, :] = jnp.where(top > 0.5 * NONE, top + jnp.log(total), NONE)


def make_table(table_ref):
    row = lax.broadcasted_iota(jnp.int32, (128, 128), 0) & 31
    for q in range(32):
        table_ref[q] = (row == q).astype(F32).astype(jnp.bfloat16)


def put_total(out_ref, mass):
    rows = out_ref.shape[0]
    total = jnp.sum(jnp.sum(mass.astype(F32), axis=0, keepdims=True), axis=1, keepdims=True)
    out_ref[rows - 8 : rows, :] = jnp.broadcast_to(jnp.log(total), (8, 128))


def first_kernel(src_list, tgt_list, count_list, start_in, mass_in, src_in, tgt_in, out, columns, slots, tops, sums, rows, wide, left, right, src_ids, tgt_ids, count, start, mass, src_coords, tgt_coords, square, table, sems):
    pairs = [(src_list, src_ids), (tgt_list, tgt_ids), (count_list, count), (start_in, start), (mass_in, mass), (src_in, src_coords), (tgt_in, tgt_coords)]
    copies = [pltpu.make_async_copy(here, there, sems.at[n]) for n, (here, there) in enumerate(pairs)]
    for copy in copies:
        copy.start()
    for copy in copies:
        copy.wait()
    make_table(table)
    squares(tgt_coords, src_coords, tgt_ids, src_ids, rows, wide, left, right, square)
    half_step(start[...], src_ids, tgt_ids, count, square, table, columns, slots, tops, sums, out)
    put_total(out, mass[...])


def square_kernel(sub_ids, lane_ids, sub_coords, lane_coords, square, rows, wide, left, right):
    squares(sub_coords, lane_coords, sub_ids, lane_ids, rows, wide, left, right, square)


def first_src_kernel(src_ids, tgt_ids, count, m0, m1, m2, m3, src_mass, square, table, out, tgt_const, columns, slots, tops, sums):
    merged = lse([m0[...], m1[...], m2[...], m3[...]])
    tgt_const[...] = merged[128:136]
    potential = jnp.log(src_mass[...].astype(F32)) - merged[0:128]
    half_step(potential, tgt_ids, src_ids, count, square, table, columns, slots, tops, sums, out)
    put_total(out, src_mass[...])


def src_kernel(src_ids, tgt_ids, count, m0, m1, m2, m3, src_mass, src_const, square, table, out, *rest):
    *pot, columns, slots, tops, sums = rest
    potential = jnp.log(src_mass[...].astype(F32)) - src_const[0:1] - lse([m0[...], m1[...], m2[...], m3[...]])
    if pot:
        pot[0][...] = potential
    half_step(potential, tgt_ids, src_ids, count, square, table, columns, slots, tops, sums, out)


def first_tgt_kernel(src_ids, tgt_ids, count, m0, m1, m2, m3, tgt_mass, tgt_const, square, table, out, src_const, columns, slots, tops, sums):
    merged = lse([m0[...], m1[...], m2[...], m3[...]])
    src_const[...] = merged[64:72]
    potential = jnp.log(tgt_mass[...].astype(F32)) - tgt_const[0:1] - (merged[0:64] - merged[64:65])
    half_step(potential, src_ids, tgt_ids, count, square, table, columns, slots, tops, sums, out)


def tgt_kernel(src_ids, tgt_ids, count, m0, m1, m2, m3, tgt_mass, tgt_const, square, table, out, columns, slots, tops, sums):
    potential = jnp.log(tgt_mass[...].astype(F32)) - tgt_const[0:1] - lse([m0[...], m1[...], m2[...], m3[...]])
    half_step(potential, src_ids, tgt_ids, count, square, table, columns, slots, tops, sums, out)


SMEM = pl.BlockSpec(memory_space=pltpu.SMEM)
VMEM = pl.BlockSpec(memory_space=pltpu.VMEM)


HBM = pl.BlockSpec(memory_space=pltpu.HBM)
PARAMS = pltpu.CompilerParams(vmem_limit_bytes=12 << 20)
SQUARES = jax.ShapeDtypeStruct((SLOTS, 128, 128), F32)


TABLE = jax.ShapeDtypeStruct((32, 128, 128), jnp.bfloat16)


def half_scratch(lane_tiles):
    sub_tiles = 192 - lane_tiles
    return [pltpu.VMEM((sub_tiles // 32, 128, 128), jnp.bfloat16), pltpu.VMEM((SLOTS * 8, 128), F32)] + [pltpu.VMEM((lane_tiles * 8, 128), F32)] * 2


def square_scratch(left_tiles, right_tiles):
    return [
        pltpu.VMEM((3, 128, 128), jnp.int32),
        pltpu.VMEM((2048, 128), F32),
        pltpu.VMEM((left_tiles // 8, 128, 128), jnp.bfloat16),
        pltpu.VMEM((right_tiles, 16, 128), jnp.bfloat16),
    ]


def first_call(*args):
    return pl.pallas_call(
        first_kernel,
        out_shape=jax.ShapeDtypeStruct((136, 128), F32),
        in_specs=[HBM] * 7,
        out_specs=VMEM,
        scratch_shapes=half_scratch(128) + square_scratch(64, 128)
        + [pltpu.SMEM(x.shape, x.dtype) for x in args[:3]]
        + [pltpu.VMEM(x.shape, x.dtype) for x in args[3:]]
        + [pltpu.VMEM(SQUARES.shape, F32), pltpu.VMEM(TABLE.shape, TABLE.dtype), pltpu.SemaphoreType.DMA((7,))],
    )(*args)


def square_call(sub_ids, lane_ids, sub_coords, lane_coords):
    return pl.pallas_call(
        square_kernel, out_shape=SQUARES, in_specs=[SMEM] * 2 + [VMEM] * 2, out_specs=VMEM,
        scratch_shapes=square_scratch(sub_coords.shape[1] // 128, lane_coords.shape[1] // 128), compiler_params=PARAMS,
    )(sub_ids, lane_ids, sub_coords, lane_coords)


def table_call():
    return pl.pallas_call(make_table, out_shape=TABLE, out_specs=VMEM, compiler_params=PARAMS)()


def call(body, lane_tiles, outs, *args):
    return pl.pallas_call(
        body,
        out_shape=[jax.ShapeDtypeStruct((rows, 128), F32) for rows in outs],
        in_specs=[SMEM] * 3 + [VMEM] * (len(args) - 3),
        out_specs=[VMEM] * len(outs),
        scratch_shapes=half_scratch(lane_tiles),
        compiler_params=PARAMS,
    )(*args)


def col_permute(value, source):
    pairs = []
    for i in range(32):
        y, z = source(i // 8, i % 8)
        pairs.append((y % 4 * 8 + z % 8, i))
    return lax.ppermute(value, "col", pairs)


def row_permute(value, shift):
    return lax.ppermute(value, "row", [(i, (i + 2 * shift) % 8) for i in range(8)])


def over_col(message):
    beside = col_permute(message, lambda y, z: (y, z ^ 1))
    corner = col_permute(message, lambda y, z: (y ^ 1, z ^ 1))
    above = col_permute(message, lambda y, z: (y ^ 1, z))
    merged = lse([message, beside, above, corner])
    merged = lse([merged, col_permute(merged, lambda y, z: (y ^ 3, z))])
    return [merged] + [col_permute(merged, lambda y, z, k=k: (y, z + k if z % 2 else z - k)) for k in (1, 3, -2)]


def over_row(message):
    other = lax.ppermute(message, "row", [(i, i ^ 1) for i in range(8)])
    merged = lse([message, other])
    ahead, behind, across = (row_permute(merged, k) for k in (1, 3, 2))
    return [merged, ahead, across, behind]


def on_device(src_coords, tgt_coords, src_mass, tgt_mass, tgt_start, kept_src, kept_tgt, kept_count):
    src_mass = src_mass.reshape(128, 128)
    tgt_mass = tgt_mass.reshape(64, 128)
    lists = (kept_src, kept_tgt, kept_count)
    message = first_call(*lists, tgt_start.reshape(64, 128), tgt_mass, src_coords, tgt_coords)
    tgt_lanes = square_call(kept_src, kept_tgt, src_coords, tgt_coords)
    table = table_call()
    src_lanes = square_call(kept_tgt, kept_src, tgt_coords, src_coords)
    for iteration in range(ITERS):
        parts = over_col(message)
        if iteration == 0:
            message, tgt_const = call(first_src_kernel, 64, [72, 8], *lists, *parts, src_mass, tgt_lanes, table)
        elif iteration + 1 < ITERS:
            (message,) = call(src_kernel, 64, [64], *lists, *parts, src_mass, src_const, tgt_lanes, table)
        else:
            message, src_potential = call(src_kernel, 64, [64, 128], *lists, *parts, src_mass, src_const, tgt_lanes, table)
        parts = over_row(message)
        if iteration == 0:
            message, src_const = call(first_tgt_kernel, 128, [128, 8], *lists, *parts, tgt_mass, tgt_const, src_lanes, table)
        elif iteration + 1 < ITERS:
            (message,) = call(tgt_kernel, 128, [128], *lists, *parts, tgt_mass, tgt_const, src_lanes, table)
    tgt_potential = jnp.log(tgt_mass.astype(F32)) - tgt_const[0:1] - lse(parts)
    return src_potential.reshape(-1), tgt_potential.reshape(-1)


def solution(mesh):
    placed = (
        P(None, "row"),
        P(None, "col"),
        P("row"),
        P("col"),
        P("col"),
        P("row", "col", None),
        P("row", "col", None),
        P("row", "col"),
    )
    return jax.shard_map(
        on_device, mesh=mesh, in_specs=placed, out_specs=(P("row"), P("col")), check_vma=False
    )
```

```python
import functools

import jax
import jax.numpy as jnp
from jax import lax
from jax.experimental import pallas as pl
from jax.experimental.pallas import tpu as pltpu
from jax.sharding import PartitionSpec as P

ITERS = 3
NONE = -1.0e30
LOG2E = 1.4426950408889634
LN2 = 0.6931471805599453
COST = 0.05 * LOG2E
SLOTS = 64
GROUP = 16
F32 = jnp.float32


def lse(parts):
    top = functools.reduce(jnp.maximum, parts)
    terms = [jnp.exp(p - top) for p in parts]
    while len(terms) > 1:
        half = len(terms) // 2
        terms = [terms[k] + terms[k + half] for k in range(half)]
    return top + jnp.log(terms[0])


def features(coords_ref, rows_ref, wide_ref, left_ref, right_ref):
    tiles = coords_ref.shape[1] // 128
    for d in range(3):
        for t in range(tiles):
            rows_ref[d, t : t + 1, :] = coords_ref[d : d + 1, t * 128 : (t + 1) * 128]
    wide_ref[0 : tiles * 16, :] = jnp.zeros((tiles * 16, 128), F32)
    for at in range(0, tiles, 8):
        x, y, z = (rows_ref[d, at : at + 8, :] for d in range(3))
        norm = x * x + y * y + z * z
        low = norm & 31
        high = norm - low
        one = jnp.ones((8, 128), F32)
        if right_ref is None:
            values = [x, y, z, high, low, one, one]
        else:
            values = [-2 * x, -2 * y, -2 * z, one, one, high, low]
        for k, value in enumerate(values):
            wide_ref[pl.ds(at * 16 + k, 8, stride=16), :] = value.astype(F32)
    if right_ref is None:
        for c in range(tiles // 8):
            left_ref[c] = wide_ref[c * 128 : (c + 1) * 128, :].T.astype(jnp.bfloat16)
    else:
        for t in range(tiles):
            right_ref[t] = wide_ref[t * 16 : (t + 1) * 16, :].astype(jnp.bfloat16)


def squares(sub_ids_ref, lane_ids_ref, left_ref, right_ref, out_ref):
    def some(g, carry):
        for u in range(GROUP):
            k = g * GROUP + u
            sub = sub_ids_ref[0, 0, k]
            block = right_ref[lane_ids_ref[0, 0, k]]
            member = sub & 7
            right = jnp.concatenate(
                [jnp.where(member == q, block, jnp.zeros_like(block)) for q in range(8)], axis=0
            )
            out_ref[k] = jnp.dot(left_ref[sub >> 3], right, preferred_element_type=F32) * COST
        return carry

    lax.fori_loop(0, SLOTS // GROUP, some, 0)


def half_step(potential, lane_ids_ref, sub_ids_ref, count_ref, square_ref, table_ref, columns_ref, slots_ref, tops_ref, sums_ref, out_ref):
    sub_tiles = potential.shape[0]
    lane_tiles = tops_ref.shape[0] // 8
    scaled = potential * LOG2E
    high = scaled.astype(jnp.bfloat16).astype(F32)
    middle = (scaled - high).astype(jnp.bfloat16).astype(F32)
    low = scaled - high - middle
    empty = jnp.zeros((32, 128), F32)
    for c in range(sub_tiles // 32):
        at = slice(c * 32, c * 32 + 32)
        columns_ref[c] = jnp.concatenate([high[at], middle[at], low[at], empty], axis=0).T.astype(jnp.bfloat16)
    count = count_ref[0, 0]
    places = [pl.ds(pl.multiple_of(lane_ids_ref[0, 0, k] * 8, 8), 8) for k in range(SLOTS)]
    tops_ref[...] = jnp.full(tops_ref.shape, NONE, jnp.float32)
    sums_ref[...] = jnp.zeros(sums_ref.shape, jnp.float32)
    for k in range(SLOTS):
        sub = sub_ids_ref[0, 0, k]
        value = jnp.dot(columns_ref[sub >> 5], table_ref[sub & 31], preferred_element_type=F32)
        score = (value - square_ref[k]).reshape(16, 8, 128)
        peak = jnp.max(score, axis=0)
        total = jnp.sum(jnp.exp2(score - peak[None]), axis=0)
        slots_ref[k * 8 : k * 8 + 8, :] = jnp.where(k < count, peak * LN2 + jnp.log(total), NONE)
    for k in range(SLOTS):
        tops_ref[places[k], :] = jnp.maximum(tops_ref[places[k], :], slots_ref[k * 8 : k * 8 + 8, :])
    for k in range(SLOTS):
        at = slice(k * 8, k * 8 + 8)
        slots_ref[at, :] = jnp.exp(slots_ref[at, :] - tops_ref[places[k], :])
    for k in range(SLOTS):
        sums_ref[places[k], :] = sums_ref[places[k], :] + slots_ref[k * 8 : k * 8 + 8, :]
    for at in range(0, lane_tiles, 8):
        tops = [tops_ref[pl.ds(at * 8 + q, 8, stride=8), :] for q in range(8)]
        sums = [sums_ref[pl.ds(at * 8 + q, 8, stride=8), :] for q in range(8)]
        top = functools.reduce(jnp.maximum, tops)
        total = functools.reduce(jnp.add, [s * jnp.exp(t - top) for t, s in zip(tops, sums)])
        out_ref[at : at + 8, :] = jnp.where(top > 0.5 * NONE, top + jnp.log(total), NONE)


def make_table(table_ref):
    row = lax.broadcasted_iota(jnp.int32, (128, 128), 0) & 31
    for q in range(32):
        table_ref[q] = (row == q).astype(F32).astype(jnp.bfloat16)


def put_total(out_ref, mass):
    rows = out_ref.shape[0]
    total = jnp.sum(jnp.sum(mass.astype(F32), axis=0, keepdims=True), axis=1, keepdims=True)
    out_ref[rows - 8 : rows, :] = jnp.broadcast_to(jnp.log(total), (8, 128))


def first_kernel(src_list, tgt_list, count_list, start_in, mass_in, src_in, tgt_in, out, columns, slots, tops, sums, rows, wide, left, right, src_ids, tgt_ids, count, start, mass, src_coords, tgt_coords, square, table, sems):
    pairs = [(src_list, src_ids), (tgt_list, tgt_ids), (count_list, count), (start_in, start), (mass_in, mass), (src_in, src_coords), (tgt_in, tgt_coords)]
    copies = [pltpu.make_async_copy(here, there, sems.at[n]) for n, (here, there) in enumerate(pairs)]
    for copy in copies:
        copy.start()
    for copy in copies:
        copy.wait()
    make_table(table)
    features(tgt_coords, rows, wide, left, None)
    features(src_coords, rows, wide, None, right)
    squares(tgt_ids, src_ids, left, right, square)
    half_step(start[...], src_ids, tgt_ids, count, square, table, columns, slots, tops, sums, out)
    put_total(out, mass[...])


def feature_kernel(sub_coords, lane_coords, left, right, rows, wide):
    features(sub_coords, rows, wide, left, None)
    features(lane_coords, rows, wide, None, right)


def first_src_kernel(src_ids, tgt_ids, count, m0, m1, m2, m3, src_mass, square, table, out, tgt_const, columns, slots, tops, sums):
    merged = lse([m0[...], m1[...], m2[...], m3[...]])
    tgt_const[...] = merged[128:136]
    potential = jnp.log(src_mass[...].astype(F32)) - merged[0:128]
    half_step(potential, tgt_ids, src_ids, count, square, table, columns, slots, tops, sums, out)
    put_total(out, src_mass[...])


def src_kernel(src_ids, tgt_ids, count, m0, m1, m2, m3, src_mass, src_const, square, table, out, *rest):
    *pot, columns, slots, tops, sums = rest
    potential = jnp.log(src_mass[...].astype(F32)) - src_const[0:1] - lse([m0[...], m1[...], m2[...], m3[...]])
    if pot:
        pot[0][...] = potential
    half_step(potential, tgt_ids, src_ids, count, square, table, columns, slots, tops, sums, out)


def first_tgt_kernel(src_ids, tgt_ids, count, m0, m1, m2, m3, tgt_mass, tgt_const, square, table, out, src_const, columns, slots, tops, sums):
    merged = lse([m0[...], m1[...], m2[...], m3[...]])
    src_const[...] = merged[64:72]
    potential = jnp.log(tgt_mass[...].astype(F32)) - tgt_const[0:1] - (merged[0:64] - merged[64:65])
    half_step(potential, src_ids, tgt_ids, count, square, table, columns, slots, tops, sums, out)


def tgt_kernel(src_ids, tgt_ids, count, m0, m1, m2, m3, tgt_mass, tgt_const, square, table, out, columns, slots, tops, sums):
    potential = jnp.log(tgt_mass[...].astype(F32)) - tgt_const[0:1] - lse([m0[...], m1[...], m2[...], m3[...]])
    half_step(potential, src_ids, tgt_ids, count, square, table, columns, slots, tops, sums, out)


SMEM = pl.BlockSpec(memory_space=pltpu.SMEM)
VMEM = pl.BlockSpec(memory_space=pltpu.VMEM)


HBM = pl.BlockSpec(memory_space=pltpu.HBM)
PARAMS = pltpu.CompilerParams(vmem_limit_bytes=12 << 20)
SQUARES = jax.ShapeDtypeStruct((SLOTS, 128, 128), F32)


TABLE = jax.ShapeDtypeStruct((32, 128, 128), jnp.bfloat16)


def half_scratch(lane_tiles):
    sub_tiles = 192 - lane_tiles
    return [pltpu.VMEM((sub_tiles // 32, 128, 128), jnp.bfloat16), pltpu.VMEM((SLOTS * 8, 128), F32)] + [pltpu.VMEM((lane_tiles * 8, 128), F32)] * 2


def square_scratch(left_tiles, right_tiles):
    return [
        pltpu.VMEM((3, 128, 128), jnp.int32),
        pltpu.VMEM((2048, 128), F32),
        pltpu.VMEM((left_tiles // 8, 128, 128), jnp.bfloat16),
        pltpu.VMEM((right_tiles, 16, 128), jnp.bfloat16),
    ]


def first_call(*args):
    return pl.pallas_call(
        first_kernel,
        out_shape=jax.ShapeDtypeStruct((136, 128), F32),
        in_specs=[HBM] * 7,
        out_specs=VMEM,
        scratch_shapes=half_scratch(128) + square_scratch(64, 128)
        + [pltpu.SMEM(x.shape, x.dtype) for x in args[:3]]
        + [pltpu.VMEM(x.shape, x.dtype) for x in args[3:]]
        + [pltpu.VMEM(SQUARES.shape, F32), pltpu.VMEM(TABLE.shape, TABLE.dtype), pltpu.SemaphoreType.DMA((7,))],
    )(*args)


def feature_call(sub_coords, lane_coords):
    rows, wide, left, right = square_scratch(sub_coords.shape[1] // 128, lane_coords.shape[1] // 128)
    return pl.pallas_call(
        feature_kernel,
        out_shape=[jax.ShapeDtypeStruct(x.shape, x.dtype) for x in (left, right)],
        in_specs=[VMEM] * 2, out_specs=[VMEM] * 2, scratch_shapes=[rows, wide], compiler_params=PARAMS,
    )(sub_coords, lane_coords)


def square_call(sub_ids, lane_ids, left, right):
    return pl.pallas_call(
        squares, out_shape=SQUARES, in_specs=[SMEM] * 2 + [VMEM] * 2, out_specs=VMEM, compiler_params=PARAMS,
    )(sub_ids, lane_ids, left, right)


def table_call():
    return pl.pallas_call(make_table, out_shape=TABLE, out_specs=VMEM, compiler_params=PARAMS)()


def call(body, lane_tiles, outs, *args):
    return pl.pallas_call(
        body,
        out_shape=[jax.ShapeDtypeStruct((rows, 128), F32) for rows in outs],
        in_specs=[SMEM] * 3 + [VMEM] * (len(args) - 3),
        out_specs=[VMEM] * len(outs),
        scratch_shapes=half_scratch(lane_tiles),
        compiler_params=PARAMS,
    )(*args)


def col_permute(value, source):
    pairs = []
    for i in range(32):
        y, z = source(i // 8, i % 8)
        pairs.append((y % 4 * 8 + z % 8, i))
    return lax.ppermute(value, "col", pairs)


def row_permute(value, shift):
    return lax.ppermute(value, "row", [(i, (i + 2 * shift) % 8) for i in range(8)])


def over_col(message, forms=None, lists=None):
    beside = col_permute(message, lambda y, z: (y, z ^ 1))
    corner = col_permute(message, lambda y, z: (y ^ 1, z ^ 1))
    above = col_permute(message, lambda y, z: (y ^ 1, z))
    if forms is not None:
        beside, corner, above, *forms = lax.optimization_barrier((beside, corner, above, *forms))
    merged = lse([message, beside, above, corner])
    other = col_permute(merged, lambda y, z: (y ^ 3, z))
    costs = None
    if forms is not None:
        other, costs = lax.optimization_barrier((other, square_call(*lists, *forms)))
    merged = lse([merged, other])
    return [merged] + [col_permute(merged, lambda y, z, k=k: (y, z + k if z % 2 else z - k)) for k in (1, 3, -2)], costs


def over_row(message):
    other = lax.ppermute(message, "row", [(i, i ^ 1) for i in range(8)])
    merged = lse([message, other])
    ahead, behind, across = (row_permute(merged, k) for k in (1, 3, 2))
    return [merged, ahead, across, behind]


def on_device(src_coords, tgt_coords, src_mass, tgt_mass, tgt_start, kept_src, kept_tgt, kept_count):
    src_mass = src_mass.reshape(128, 128)
    tgt_mass = tgt_mass.reshape(64, 128)
    lists = (kept_src, kept_tgt, kept_count)
    message = first_call(*lists, tgt_start.reshape(64, 128), tgt_mass, src_coords, tgt_coords)
    table = table_call()
    src_lanes = square_call(kept_tgt, kept_src, *feature_call(tgt_coords, src_coords))
    for iteration in range(ITERS):
        if iteration == 0:
            parts, tgt_lanes = over_col(message, feature_call(src_coords, tgt_coords), (kept_src, kept_tgt))
            message, tgt_const = call(first_src_kernel, 64, [72, 8], *lists, *parts, src_mass, tgt_lanes, table)
        elif iteration + 1 < ITERS:
            parts, _ = over_col(message)
            (message,) = call(src_kernel, 64, [64], *lists, *parts, src_mass, src_const, tgt_lanes, table)
        else:
            parts, _ = over_col(message)
            message, src_potential = call(src_kernel, 64, [64, 128], *lists, *parts, src_mass, src_const, tgt_lanes, table)
        parts = over_row(message)
        if iteration == 0:
            message, src_const = call(first_tgt_kernel, 128, [128, 8], *lists, *parts, tgt_mass, tgt_const, src_lanes, table)
        elif iteration + 1 < ITERS:
            (message,) = call(tgt_kernel, 128, [128], *lists, *parts, tgt_mass, tgt_const, src_lanes, table)
    tgt_potential = jnp.log(tgt_mass.astype(F32)) - tgt_const[0:1] - lse(parts)
    return src_potential.reshape(-1), tgt_potential.reshape(-1)


def solution(mesh):
    placed = (
        P(None, "row"),
        P(None, "col"),
        P("row"),
        P("col"),
        P("col"),
        P("row", "col", None),
        P("row", "col", None),
        P("row", "col"),
    )
    return jax.shard_map(
        on_device, mesh=mesh, in_specs=placed, out_specs=(P("row"), P("col")), check_vma=False
    )
```

```python
import functools

import jax
import jax.numpy as jnp
from jax import lax
from jax.experimental import pallas as pl
from jax.experimental.pallas import tpu as pltpu
from jax.sharding import PartitionSpec as P

ITERS = 3
NONE = -1.0e30
LOG2E = 1.4426950408889634
LN2 = 0.6931471805599453
COST = 0.05 * LOG2E
SLOTS = 64
GROUP = 16
F32 = jnp.float32


def lse(parts):
    top = functools.reduce(jnp.maximum, parts)
    terms = [jnp.exp(p - top) for p in parts]
    while len(terms) > 1:
        half = len(terms) // 2
        terms = [terms[k] + terms[k + half] for k in range(half)]
    return top + jnp.log(terms[0])


def features(coords_ref, rows_ref, wide_ref, left_ref, right_ref):
    tiles = coords_ref.shape[1] // 128
    for d in range(3):
        for t in range(tiles):
            rows_ref[d, t : t + 1, :] = coords_ref[d : d + 1, t * 128 : (t + 1) * 128]
    wide_ref[0 : tiles * 16, :] = jnp.zeros((tiles * 16, 128), F32)
    for at in range(0, tiles, 8):
        x, y, z = (rows_ref[d, at : at + 8, :] for d in range(3))
        norm = x * x + y * y + z * z
        low = norm & 31
        high = norm - low
        one = jnp.ones((8, 128), F32)
        if right_ref is None:
            values = [x, y, z, high, low, one, one]
        else:
            values = [-2 * x, -2 * y, -2 * z, one, one, high, low]
        for k, value in enumerate(values):
            wide_ref[pl.ds(at * 16 + k, 8, stride=16), :] = value.astype(F32)
    if right_ref is None:
        for c in range(tiles // 8):
            left_ref[c] = wide_ref[c * 128 : (c + 1) * 128, :].T.astype(jnp.bfloat16)
    else:
        for t in range(tiles):
            right_ref[t] = wide_ref[t * 16 : (t + 1) * 16, :].astype(jnp.bfloat16)


def squares(sub_ids_ref, lane_ids_ref, left_ref, right_ref, out_ref):
    def some(g, carry):
        for u in range(GROUP):
            k = g * GROUP + u
            sub = sub_ids_ref[0, 0, k]
            block = right_ref[lane_ids_ref[0, 0, k]]
            member = sub & 7
            right = jnp.concatenate(
                [jnp.where(member == q, block, jnp.zeros_like(block)) for q in range(8)], axis=0
            )
            out_ref[k] = jnp.dot(left_ref[sub >> 3], right, preferred_element_type=F32) * COST
        return carry

    lax.fori_loop(0, SLOTS // GROUP, some, 0)


def half_step(potential, lane_ids_ref, sub_ids_ref, count_ref, square_ref, table_ref, columns_ref, slots_ref, tops_ref, sums_ref, out_ref):
    sub_tiles = potential.shape[0]
    lane_tiles = tops_ref.shape[0] // 8
    scaled = potential * LOG2E
    high = scaled.astype(jnp.bfloat16).astype(F32)
    middle = (scaled - high).astype(jnp.bfloat16).astype(F32)
    low = scaled - high - middle
    empty = jnp.zeros((32, 128), F32)
    for c in range(sub_tiles // 32):
        at = slice(c * 32, c * 32 + 32)
        columns_ref[c] = jnp.concatenate([high[at], middle[at], low[at], empty], axis=0).T.astype(jnp.bfloat16)
    count = count_ref[0, 0]
    places = [pl.ds(pl.multiple_of(lane_ids_ref[0, 0, k] * 8, 8), 8) for k in range(SLOTS)]
    tops_ref[...] = jnp.full(tops_ref.shape, NONE, jnp.float32)
    sums_ref[...] = jnp.zeros(sums_ref.shape, jnp.float32)
    for k in range(SLOTS):
        sub = sub_ids_ref[0, 0, k]
        value = jnp.dot(columns_ref[sub >> 5], table_ref[sub & 31], preferred_element_type=F32)
        score = (value - square_ref[k]).reshape(16, 8, 128)
        peak = jnp.max(score, axis=0)
        total = jnp.sum(jnp.exp2(score - peak[None]), axis=0)
        slots_ref[k * 8 : k * 8 + 8, :] = jnp.where(k < count, peak * LN2 + jnp.log(total), NONE)
    for k in range(SLOTS):
        tops_ref[places[k], :] = jnp.maximum(tops_ref[places[k], :], slots_ref[k * 8 : k * 8 + 8, :])
    for k in range(SLOTS):
        at = slice(k * 8, k * 8 + 8)
        slots_ref[at, :] = jnp.exp(slots_ref[at, :] - tops_ref[places[k], :])
    for k in range(SLOTS):
        sums_ref[places[k], :] = sums_ref[places[k], :] + slots_ref[k * 8 : k * 8 + 8, :]
    for at in range(0, lane_tiles, 8):
        tops = [tops_ref[pl.ds(at * 8 + q, 8, stride=8), :] for q in range(8)]
        sums = [sums_ref[pl.ds(at * 8 + q, 8, stride=8), :] for q in range(8)]
        top = functools.reduce(jnp.maximum, tops)
        total = functools.reduce(jnp.add, [s * jnp.exp(t - top) for t, s in zip(tops, sums)])
        out_ref[at : at + 8, :] = jnp.where(top > 0.5 * NONE, top + jnp.log(total), NONE)


def make_table(table_ref):
    row = lax.broadcasted_iota(jnp.int32, (128, 128), 0) & 31
    for q in range(32):
        table_ref[q] = (row == q).astype(F32).astype(jnp.bfloat16)


def put_total(out_ref, mass):
    rows = out_ref.shape[0]
    total = jnp.sum(jnp.sum(mass.astype(F32), axis=0, keepdims=True), axis=1, keepdims=True)
    out_ref[rows - 8 : rows, :] = jnp.broadcast_to(jnp.log(total), (8, 128))


def first_kernel(src_list, tgt_list, count_list, start_in, mass_in, src_in, tgt_in, out, columns, slots, tops, sums, rows, wide, left, right, src_ids, tgt_ids, count, start, mass, src_coords, tgt_coords, square, table, sems):
    pairs = [(src_list, src_ids), (tgt_list, tgt_ids), (count_list, count), (start_in, start), (mass_in, mass), (src_in, src_coords), (tgt_in, tgt_coords)]
    copies = [pltpu.make_async_copy(here, there, sems.at[n]) for n, (here, there) in enumerate(pairs)]
    for copy in copies:
        copy.start()
    make_table(table)
    copies[6].wait()
    features(tgt_coords, rows, wide, left, None)
    copies[5].wait()
    features(src_coords, rows, wide, None, right)
    for copy in copies[:5]:
        copy.wait()
    squares(tgt_ids, src_ids, left, right, square)
    half_step(start[...], src_ids, tgt_ids, count, square, table, columns, slots, tops, sums, out)
    put_total(out, mass[...])


def feature_kernel(sub_coords, lane_coords, left, right, rows, wide):
    features(sub_coords, rows, wide, left, None)
    features(lane_coords, rows, wide, None, right)


def first_src_kernel(src_ids, tgt_ids, count, m0, m1, m2, m3, src_mass, square, table, out, tgt_const, columns, slots, tops, sums):
    merged = lse([m0[...], m1[...], m2[...], m3[...]])
    tgt_const[...] = merged[128:136]
    potential = jnp.log(src_mass[...].astype(F32)) - merged[0:128]
    half_step(potential, tgt_ids, src_ids, count, square, table, columns, slots, tops, sums, out)
    put_total(out, src_mass[...])


def src_kernel(src_ids, tgt_ids, count, m0, m1, m2, m3, src_mass, src_const, square, table, out, *rest):
    *pot, columns, slots, tops, sums = rest
    potential = jnp.log(src_mass[...].astype(F32)) - src_const[0:1] - lse([m0[...], m1[...], m2[...], m3[...]])
    if pot:
        pot[0][...] = potential
    half_step(potential, tgt_ids, src_ids, count, square, table, columns, slots, tops, sums, out)


def first_tgt_kernel(src_ids, tgt_ids, count, m0, m1, m2, m3, tgt_mass, tgt_const, square, table, out, src_const, columns, slots, tops, sums):
    merged = lse([m0[...], m1[...], m2[...], m3[...]])
    src_const[...] = merged[64:72]
    potential = jnp.log(tgt_mass[...].astype(F32)) - tgt_const[0:1] - (merged[0:64] - merged[64:65])
    half_step(potential, src_ids, tgt_ids, count, square, table, columns, slots, tops, sums, out)


def tgt_kernel(src_ids, tgt_ids, count, m0, m1, m2, m3, tgt_mass, tgt_const, square, table, out, columns, slots, tops, sums):
    potential = jnp.log(tgt_mass[...].astype(F32)) - tgt_const[0:1] - lse([m0[...], m1[...], m2[...], m3[...]])
    half_step(potential, src_ids, tgt_ids, count, square, table, columns, slots, tops, sums, out)


SMEM = pl.BlockSpec(memory_space=pltpu.SMEM)
VMEM = pl.BlockSpec(memory_space=pltpu.VMEM)


HBM = pl.BlockSpec(memory_space=pltpu.HBM)
PARAMS = pltpu.CompilerParams(vmem_limit_bytes=12 << 20)
SQUARES = jax.ShapeDtypeStruct((SLOTS, 128, 128), F32)


TABLE = jax.ShapeDtypeStruct((32, 128, 128), jnp.bfloat16)


def half_scratch(lane_tiles):
    sub_tiles = 192 - lane_tiles
    return [pltpu.VMEM((sub_tiles // 32, 128, 128), jnp.bfloat16), pltpu.VMEM((SLOTS * 8, 128), F32)] + [pltpu.VMEM((lane_tiles * 8, 128), F32)] * 2


def square_scratch(left_tiles, right_tiles):
    return [
        pltpu.VMEM((3, 128, 128), jnp.int32),
        pltpu.VMEM((2048, 128), F32),
        pltpu.VMEM((left_tiles // 8, 128, 128), jnp.bfloat16),
        pltpu.VMEM((right_tiles, 16, 128), jnp.bfloat16),
    ]


def first_call(*args):
    return pl.pallas_call(
        first_kernel,
        out_shape=jax.ShapeDtypeStruct((136, 128), F32),
        in_specs=[HBM] * 7,
        out_specs=VMEM,
        scratch_shapes=half_scratch(128) + square_scratch(64, 128)
        + [pltpu.SMEM(x.shape, x.dtype) for x in args[:3]]
        + [pltpu.VMEM(x.shape, x.dtype) for x in args[3:]]
        + [pltpu.VMEM(SQUARES.shape, F32), pltpu.VMEM(TABLE.shape, TABLE.dtype), pltpu.SemaphoreType.DMA((7,))],
    )(*args)


def feature_call(sub_coords, lane_coords):
    rows, wide, left, right = square_scratch(sub_coords.shape[1] // 128, lane_coords.shape[1] // 128)
    return pl.pallas_call(
        feature_kernel,
        out_shape=[jax.ShapeDtypeStruct(x.shape, x.dtype) for x in (left, right)],
        in_specs=[VMEM] * 2, out_specs=[VMEM] * 2, scratch_shapes=[rows, wide], compiler_params=PARAMS,
    )(sub_coords, lane_coords)


def square_call(sub_ids, lane_ids, left, right):
    return pl.pallas_call(
        squares, out_shape=SQUARES, in_specs=[SMEM] * 2 + [VMEM] * 2, out_specs=VMEM, compiler_params=PARAMS,
    )(sub_ids, lane_ids, left, right)


def table_call():
    return pl.pallas_call(make_table, out_shape=TABLE, out_specs=VMEM, compiler_params=PARAMS)()


def call(body, lane_tiles, outs, *args):
    return pl.pallas_call(
        body,
        out_shape=[jax.ShapeDtypeStruct((rows, 128), F32) for rows in outs],
        in_specs=[SMEM] * 3 + [VMEM] * (len(args) - 3),
        out_specs=[VMEM] * len(outs),
        scratch_shapes=half_scratch(lane_tiles),
        compiler_params=PARAMS,
    )(*args)


def col_permute(value, source):
    pairs = []
    for i in range(32):
        y, z = source(i // 8, i % 8)
        pairs.append((y % 4 * 8 + z % 8, i))
    return lax.ppermute(value, "col", pairs)


def row_permute(value, shift):
    return lax.ppermute(value, "row", [(i, (i + 2 * shift) % 8) for i in range(8)])


def over_col(message, forms=None, lists=None):
    beside = col_permute(message, lambda y, z: (y, z ^ 1))
    corner = col_permute(message, lambda y, z: (y ^ 1, z ^ 1))
    above = col_permute(message, lambda y, z: (y ^ 1, z))
    if forms is not None:
        beside, corner, above, *forms = lax.optimization_barrier((beside, corner, above, *forms))
    merged = lse([message, beside, above, corner])
    other = col_permute(merged, lambda y, z: (y ^ 3, z))
    costs = None
    if forms is not None:
        other, costs = lax.optimization_barrier((other, square_call(*lists, *forms)))
    merged = lse([merged, other])
    return [merged] + [col_permute(merged, lambda y, z, k=k: (y, z + k if z % 2 else z - k)) for k in (1, 3, -2)], costs


def over_row(message):
    other = lax.ppermute(message, "row", [(i, i ^ 1) for i in range(8)])
    merged = lse([message, other])
    ahead, behind, across = (row_permute(merged, k) for k in (1, 3, 2))
    return [merged, ahead, across, behind]


def on_device(src_coords, tgt_coords, src_mass, tgt_mass, tgt_start, kept_src, kept_tgt, kept_count):
    src_mass = src_mass.reshape(128, 128)
    tgt_mass = tgt_mass.reshape(64, 128)
    lists = (kept_src, kept_tgt, kept_count)
    message = first_call(*lists, tgt_start.reshape(64, 128), tgt_mass, src_coords, tgt_coords)
    table = table_call()
    src_lanes = square_call(kept_tgt, kept_src, *feature_call(tgt_coords, src_coords))
    for iteration in range(ITERS):
        if iteration == 0:
            parts, tgt_lanes = over_col(message, feature_call(src_coords, tgt_coords), (kept_src, kept_tgt))
            message, tgt_const = call(first_src_kernel, 64, [72, 8], *lists, *parts, src_mass, tgt_lanes, table)
        elif iteration + 1 < ITERS:
            parts, _ = over_col(message)
            (message,) = call(src_kernel, 64, [64], *lists, *parts, src_mass, src_const, tgt_lanes, table)
        else:
            parts, _ = over_col(message)
            message, src_potential = call(src_kernel, 64, [64, 128], *lists, *parts, src_mass, src_const, tgt_lanes, table)
        parts = over_row(message)
        if iteration == 0:
            message, src_const = call(first_tgt_kernel, 128, [128, 8], *lists, *parts, tgt_mass, tgt_const, src_lanes, table)
        elif iteration + 1 < ITERS:
            (message,) = call(tgt_kernel, 128, [128], *lists, *parts, tgt_mass, tgt_const, src_lanes, table)
    tgt_potential = jnp.log(tgt_mass.astype(F32)) - tgt_const[0:1] - lse(parts)
    return src_potential.reshape(-1), tgt_potential.reshape(-1)


def solution(mesh):
    placed = (
        P(None, "row"),
        P(None, "col"),
        P("row"),
        P("col"),
        P("col"),
        P("row", "col", None),
        P("row", "col", None),
        P("row", "col"),
    )
    return jax.shard_map(
        on_device, mesh=mesh, in_specs=placed, out_specs=(P("row"), P("col")), check_vma=False
    )
```
